32 devices in a mesh: cls: 32 (over z, y, x, core), rot: 1.
Axes of the slice: x: 2, y: 2, z: 4, core: 2. Of those that a mesh axis runs over, the one named last changes fastest.
Arguments:
- particles: bfloat16 [2048, 32, 128], P(('cls', 'rot')), may hold values from -6 to 6
- panels: bfloat16 [32, 128, 32, 128], P('cls', 'rot'), may hold values from -6 to 6
- classes: int32 [2, 2048, 1], P(None, ('cls', 'rot')), may hold values from 0 to 31; in each aligned block of 64 rows (0 to 63, 64 to 127, ..., all dimensions but the last counted through in order) at most 4 rows name the same one
- candidates: int32 [2, 2048, 2], P(None, ('cls', 'rot')), may hold values from 0 to 127, all different within a row
- weights: float32 [2, 2048, 2], P(None, ('cls', 'rot')), may hold values from 0.05 to 1
- tilt_low: int32 [2048], P(('cls', 'rot')), may hold values from -16 to -6
- tilt_high: int32 [2048], P(('cls', 'rot')), may hold values from 6 to 16
Outputs:
- scores: float32 [2, 2048, 2], P(None, ('cls', 'rot'))
- new_panels: bfloat16 [32, 128, 32, 128], P('cls', 'rot')
The draws below stay inside these ranges and needn't reach their ends.
Inputs may be any that keep to these rules, and one draw needn't show every extreme that they name: `classes`: among the rows of one device in one iteration no class is named more than 4 times; in some device's rows a class is named exactly 4 times. `candidates`: the 2 orientations of a particle in one iteration are different.
All inputs are finite; a program needn't handle non-finite values.
Results may differ from the reference program's by a relative error of at most 0.007.
Values may be sent and summed in bfloat16 or wider, within the bound.
A program may use at most 64 MiB of HBM per device.

```python
import math
import jax
import jax.numpy as jnp
import numpy as np
from jax import lax

BOX = 64
BAND = 16
SHIFTS = 16
ORIENT = 128
NCAND = 2
ITERS = 2
PART_DEV = 64
CAP = 4
NCLS = 32
PARTICLES = 2048
N_CLS = 32
N_ROT = 1


def place_ends(result, key, least, top_value):
    longest = result.shape.index(max(result.shape))
    spots = []
    for shift in (0, 1):
        where = [jax.random.randint(jax.random.fold_in(key, axis), (), 0, length) for axis, length in enumerate(result.shape)]
        where[longest] = (where[longest] + shift) % result.shape[longest]
        spots.append(tuple(where))
    return result.at[spots[0]].set(least).at[spots[1]].set(top_value)


def steps_of(own_key, shape, cuts, least, largest):
    def one(position, parts):
        heights = jax.random.uniform(jax.random.fold_in(jax.random.fold_in(own_key, 6), position), (parts,), jnp.float32, least / len(cuts), largest / len(cuts))
        return jnp.repeat(jnp.exp(heights), shape[position] // parts).reshape((-1,) + (1,) * (len(shape) - position - 1))

    loudness = one(*cuts[0])
    for cut in cuts[1:]:
        loudness = loudness * one(*cut)
    return loudness


def picks_of(own_key, rows, count, top, lift):
    ranking = jax.random.permutation(jax.random.fold_in(own_key, 1), count)
    boost = ranking
    for power in range(3):
        boost = boost * boost // count
    boost = boost * lift // count
    lots = jax.random.randint(jax.random.fold_in(own_key, 2), (rows, count), 0, 4096) + boost
    fixed_rows = jax.random.permutation(jax.random.fold_in(own_key, 3), rows)[jnp.arange(count) % rows]
    lots = jnp.where(jnp.arange(rows)[:, None] == fixed_rows[None, :], 1 << 14, lots)
    priority = lots * count + jnp.arange(count)
    return lax.top_k(priority.astype(jnp.int32), top)[1].astype(jnp.int32)


def deal_out(stream_key, own, number, rows, count, top, most, lean):
    ranking = jax.random.permutation(stream_key, count)
    crowded, usual = portions_of(count, rows * top, most, lean, True), portions_of(count, rows * top, most, lean, False)
    places = jnp.arange(count)

    def named(lengths, rotation):
        used = int((lengths > 0).sum())
        fixed = max(1, used // 4)
        passed = fixed + (places - fixed + rotation * (used - fixed)) % max(1, count - fixed)
        return jnp.zeros((count,), jnp.int32).at[ranking[jnp.where(places < fixed, places, passed)]].set(jnp.asarray(lengths, jnp.int32))

    lengths = jnp.where(number % 4 == 0, named(crowded, number // 4), named(usual, number - number // 4 - 1))
    mixed = jax.random.permutation(jax.random.fold_in(own, 3), count)
    giver, sink = mixed[0:count // 2 * 2:2], mixed[1:count // 2 * 2:2]
    room = jnp.minimum(lengths[giver] - 1, most - lengths[sink]) // 2
    room = jnp.where((giver == ranking[0]) | (sink == ranking[0]) | (lengths[sink] == 0), 0, jnp.maximum(room, 0))
    passed = jax.random.randint(jax.random.fold_in(own, 4), (count // 2,), 0, 1 << 20) % (room + 1)
    lengths = lengths.at[giver].add(-passed).at[sink].add(passed)
    items = jnp.searchsorted(jnp.cumsum(lengths), jnp.arange(rows * top), side="right").astype(jnp.int32)
    grid = items.reshape(top, rows).T
    grid = grid[jax.random.permutation(jax.random.fold_in(own, 1), rows)]
    rotation = jax.random.randint(jax.random.fold_in(own, 2), (rows, 1), 0, top)
    return jnp.take_along_axis(grid, (jnp.arange(top)[None, :] + rotation) % top, axis=1)


def portions_of(amount, total, bound, skew, full):
    portions = [(1 << 20) // math.isqrt(rank ** skew) + 1 for rank in range(1, amount + 1)]
    largest = bound if full else min(bound, max(-(-total // amount), total * portions[0] // sum(portions)))
    least = 1 if total - largest >= amount - 1 else 0
    counts, surplus = [largest] + [least] * (amount - 1), total - largest - least * (amount - 1)
    while surplus > 0:
        free = [i for i in range(1, amount) if counts[i] < largest] or [i for i in range(1, amount) if counts[i] < bound]
        mass, budget = sum([portions[i] for i in free]), surplus
        for i in free:
            addition = min(bound - counts[i], max(1, budget * portions[i] // mass), surplus)
            counts[i] = counts[i] + addition
            surplus = surplus - addition
    return np.array(counts)


def scatter_about(key, dims, width, limit, cuts=(), held_as=jnp.bfloat16):
    values = width * jax.random.normal(key, dims, jnp.float32)
    if cuts:
        values = values * steps_of(key, dims, cuts, -0.22, 0.18)
    return jnp.clip(values, -limit, limit).astype(held_as)


def setup_inputs(seed: int = 0) -> dict:
    arg_keys = jax.random.split(jax.random.key(seed), 8)
    particles = scatter_about(arg_keys[0], (PARTICLES, 2 * BAND, BAND * (BAND // 2)), 1.0, 6.0, ((0, 32),))
    panels = scatter_about(arg_keys[1], (NCLS, ORIENT, 2 * BAND, BAND * (BAND // 2)), 1.0, 6.0, ((0, 32),))
    classes_keys = jax.random.split(jax.random.fold_in(arg_keys[2], 1), ITERS * PARTICLES // PART_DEV)
    classes_turns = jax.random.permutation(jax.random.fold_in(arg_keys[2], 3), ITERS * PARTICLES // PART_DEV)
    classes = jax.vmap(lambda own, number: deal_out(jax.random.fold_in(arg_keys[2], 2), own, number, PART_DEV, NCLS, 1, CAP, 2))(classes_keys, classes_turns).reshape((ITERS, PARTICLES, 1))
    candidates = picks_of(arg_keys[3], ITERS * PARTICLES, ORIENT, NCAND, 128).reshape((ITERS, PARTICLES, NCAND))
    weights = jnp.clip(jnp.exp(math.log(1.0) - 2.9957323 * jax.random.uniform(arg_keys[4], (ITERS, PARTICLES, NCAND), jnp.float32) ** steps_of(arg_keys[4], (ITERS, PARTICLES, NCAND), ((1, 32),), -0.2, 0.2)), 0.05, 1.0)
    tilt_low = place_ends(jax.random.randint(arg_keys[5], (PARTICLES,), -16, -5), jax.random.fold_in(arg_keys[5], 1), -16, (-5) - 1).astype(jnp.int32)
    tilt_high = place_ends(jax.random.randint(arg_keys[6], (PARTICLES,), 6, 17), jax.random.fold_in(arg_keys[6], 1), 6, 16).astype(jnp.int32)
    return {"particles": particles, "panels": panels, "classes": classes, "candidates": candidates, "weights": weights, "tilt_low": tilt_low, "tilt_high": tilt_high}


score_gain = 16.0
highest = lax.Precision.HIGHEST

def phase_tables(band_size, shift_count):
    frequency = jnp.arange(band_size, dtype=jnp.float32) - float(band_size // 2)
    offsets = jnp.arange(shift_count, dtype=jnp.float32) - float(shift_count // 2)
    radians = 2.0 * math.pi / BOX
    planar = radians * frequency[:, None] * offsets[None, :]
    depth_freq = jnp.arange(band_size // 2, dtype=jnp.float32)
    hermite = jnp.where(depth_freq == 0.0, 1.0, 2.0).astype(jnp.float32)
    depth_angle = radians * depth_freq[:, None] * offsets[None, :]
    return (jnp.cos(planar), jnp.sin(planar), hermite[:, None] * jnp.cos(depth_angle), hermite[:, None] * jnp.sin(depth_angle), hermite)

def wedge_mask(tilt_lower, tilt_upper, band_size):
    across_freq = jnp.arange(band_size, dtype=jnp.int32) - band_size // 2
    depth_index = jnp.arange(band_size // 2, dtype=jnp.int32)
    flipped = across_freq[:, None] < 0
    across = jnp.where(flipped, -across_freq[:, None], across_freq[:, None])
    along_depth = jnp.where(flipped, -depth_index[None, :], depth_index[None, :])
    lower_ok = tilt_lower[:, None, None] * across[None] <= 8 * along_depth[None]
    upper_ok = 8 * along_depth[None] <= tilt_upper[:, None, None] * across[None]
    return jnp.where(lower_ok & upper_ok, 1.0, 0.0).astype(jnp.float32)

def multiply(form, left, right):
    return jnp.einsum(form, left.astype(jnp.float32), right.astype(jnp.float32), precision=highest)

def section(form, left_real, left_imag, cos_table, sin_table):
    real_part = multiply(form, left_real, cos_table) - multiply(form, left_imag, sin_table)
    imag_part = multiply(form, left_real, sin_table) + multiply(form, left_imag, cos_table)
    return (real_part, imag_part)

def correlate(records, references, wedges):
    pair_count = records.shape[0]
    band_size = records.shape[1] // 2
    half_band = band_size // 2
    plane_cos, plane_sin, depth_cos, depth_sin, hermite = phase_tables(band_size, SHIFTS)
    plane_cos = plane_cos.astype(jnp.bfloat16)
    plane_sin = plane_sin.astype(jnp.bfloat16)
    depth_cos = depth_cos.astype(jnp.bfloat16)
    depth_sin = depth_sin.astype(jnp.bfloat16)
    signal = jnp.transpose(records.astype(jnp.float32).reshape(pair_count, 2, band_size, band_size, half_band), (1, 2, 3, 4, 0))
    template = jnp.transpose(references.astype(jnp.float32).reshape(pair_count, 2, band_size, band_size, half_band), (1, 2, 3, 4, 0))
    coverage = jnp.transpose(wedges, (1, 2, 0))[:, None, :, :]
    prod_real = (coverage * (signal[0] * template[0] + signal[1] * template[1])).astype(jnp.bfloat16)
    prod_imag = (coverage * (signal[0] * template[1] - signal[1] * template[0])).astype(jnp.bfloat16)
    weighting = hermite[None, None, :, None] * coverage
    signal_norm = lax.optimization_barrier(jnp.sum(weighting * (signal[0] * signal[0] + signal[1] * signal[1]), axis=(0, 1, 2)))
    template_norm = lax.optimization_barrier(jnp.sum(weighting * (template[0] * template[0] + template[1] * template[1]), axis=(0, 1, 2)))
    first_real, first_imag = section('abcn,as->sbcn', prod_real, prod_imag, plane_cos, plane_sin)
    second_real, second_imag = section('sbcn,bt->stcn', first_real.astype(jnp.bfloat16), first_imag.astype(jnp.bfloat16), plane_cos, plane_sin)
    correlation = multiply('stcn,cu->stun', second_real.astype(jnp.bfloat16), depth_cos) - multiply('stcn,cu->stun', second_imag.astype(jnp.bfloat16), depth_sin)
    summit = lax.optimization_barrier(jnp.max(correlation.reshape(-1, pair_count), axis=0))
    return score_gain * summit * lax.rsqrt(signal_norm * template_norm + 1e-06)

def score_pairs(records, panel_table, wedges, indices, block_limit):
    row_count = indices.shape[0]
    tried_count = indices.shape[1]
    pair_count = row_count * tried_count
    block_size = math.gcd(pair_count, block_limit)
    flat_index = indices.reshape(pair_count)

    def one_block(block_index):
        start_pair = block_index * block_size
        chosen = lax.dynamic_slice_in_dim(flat_index, start_pair, block_size)
        source_rows = (start_pair + jnp.arange(block_size, dtype=jnp.int32)) // tried_count
        return correlate(jnp.take(records, source_rows, axis=0), jnp.take(panel_table, chosen, axis=0), jnp.take(wedges, source_rows, axis=0))
    blocks = jnp.arange(pair_count // block_size, dtype=jnp.int32)
    return lax.map(one_block, blocks).reshape(row_count, tried_count)

def renew(tables, numerator, denominator):
    entries = tables.shape[0]
    band_size = tables.shape[1] // 2
    half_band = band_size // 2
    summed = (tables.astype(jnp.float32) + numerator).reshape(entries, 2, band_size, band_size, half_band)
    divisor = 1.0 + denominator.reshape(entries, 1, band_size, 1, half_band)
    return (summed / divisor).reshape(tables.shape).astype(jnp.bfloat16)

def round_trip(values):
    return lax.optimization_barrier(values.astype(jnp.bfloat16)).astype(jnp.float32)

def rot_partials(masked, coverage_flat, weight_sent, indices):
    entries = NCLS * ORIENT

    def by_group(carry, pieces):
        numer_sum, denom_sum = carry
        piece_data, piece_cover, piece_weight, piece_index = pieces
        numer_part = jnp.zeros((entries,) + piece_data.shape[1:], jnp.float32)
        denom_part = jnp.zeros((entries,) + piece_cover.shape[1:], jnp.float32)
        for tried_index in range(NCAND):
            numer_part = numer_part + jax.ops.segment_sum(piece_weight[:, tried_index, None, None] * piece_data, piece_index[:, tried_index], num_segments=entries)
            denom_part = denom_part + jax.ops.segment_sum(piece_weight[:, tried_index, None] * piece_cover, piece_index[:, tried_index], num_segments=entries)
        return ((numer_sum + round_trip(numer_part), denom_sum + round_trip(denom_part)), None)

    def regroup(values):
        shaped = values.reshape((N_CLS, N_ROT, PART_DEV) + values.shape[1:])
        return jnp.swapaxes(shaped, 0, 1).reshape((N_ROT, N_CLS * PART_DEV) + values.shape[1:])
    initial = (jnp.zeros((entries,) + masked.shape[1:], jnp.float32), jnp.zeros((entries,) + coverage_flat.shape[1:], jnp.float32))
    totals, unused = lax.scan(by_group, initial, (regroup(masked), regroup(coverage_flat), regroup(weight_sent), regroup(indices)))
    return totals

def reference(particles, panels, classes, candidates, weights, tilt_low, tilt_high):
    band_size = particles.shape[1] // 2
    half_band = band_size // 2
    wedges = wedge_mask(tilt_low, tilt_high, band_size)
    spread = jnp.broadcast_to(wedges[:, :, None, :], (PARTICLES, band_size, band_size, half_band)).reshape(PARTICLES, band_size, band_size * half_band)
    masked = particles.astype(jnp.float32) * jnp.concatenate([spread, spread], axis=1)
    coverage_flat = wedges.reshape(PARTICLES, band_size * half_band)
    tables = panels.reshape(NCLS * ORIENT, 2 * band_size, band_size * half_band)
    results = []
    for iteration in range(ITERS):
        indices = (classes[iteration, :, 0][:, None] * ORIENT + candidates[iteration]).astype(jnp.int32)
        results.append(score_pairs(particles, tables, wedges, indices, 1024))
        weight_sent = round_trip(weights[iteration])
        numer_sum, denom_sum = rot_partials(masked, coverage_flat, weight_sent, indices)
        tables = renew(tables, numer_sum, denom_sum)
    return (jnp.stack(results), tables.reshape(panels.shape))
```

```python
import functools
import math

import jax
import jax.numpy as jnp
import numpy as np
from jax import lax
from jax.experimental import pallas as pl
from jax.experimental.pallas import tpu as pltpu
from jax.sharding import PartitionSpec as P

BOX = 64
SHIFTS = 16
ORIENT = 128
NCAND = 2
ITERS = 2


score_gain = 16.0
highest = lax.Precision.HIGHEST


def phase_tables(band_size, shift_count):
    frequency = jnp.arange(band_size, dtype=jnp.float32) - float(band_size // 2)
    offsets = jnp.arange(shift_count, dtype=jnp.float32) - float(shift_count // 2)
    radians = 2.0 * math.pi / BOX
    planar = radians * frequency[:, None] * offsets[None, :]
    depth_freq = jnp.arange(band_size // 2, dtype=jnp.float32)
    hermite = jnp.where(depth_freq == 0.0, 1.0, 2.0).astype(jnp.float32)
    depth_angle = radians * depth_freq[:, None] * offsets[None, :]
    return (
        jnp.cos(planar),
        jnp.sin(planar),
        hermite[:, None] * jnp.cos(depth_angle),
        hermite[:, None] * jnp.sin(depth_angle),
        hermite,
    )


def wedge_mask(tilt_lower, tilt_upper, band_size):
    across_freq = jnp.arange(band_size, dtype=jnp.int32) - band_size // 2
    depth_index = jnp.arange(band_size // 2, dtype=jnp.int32)
    flipped = across_freq[:, None] < 0
    across = jnp.where(flipped, -across_freq[:, None], across_freq[:, None])
    along_depth = jnp.where(flipped, -depth_index[None, :], depth_index[None, :])
    lower_ok = tilt_lower[:, None, None] * across[None] <= 8 * along_depth[None]
    upper_ok = 8 * along_depth[None] <= tilt_upper[:, None, None] * across[None]
    return jnp.where(lower_ok & upper_ok, 1.0, 0.0).astype(jnp.float32)


def multiply(form, left, right):
    return jnp.einsum(form, left, right, preferred_element_type=jnp.float32)


def section(form, left_real, left_imag, cos_table, sin_table):
    real_part = multiply(form, left_real, cos_table) - multiply(form, left_imag, sin_table)
    imag_part = multiply(form, left_real, sin_table) + multiply(form, left_imag, cos_table)
    return (real_part, imag_part)


def correlate(records, references, wedges):
    pair_count = records.shape[0]
    band_size = records.shape[1] // 2
    half_band = band_size // 2
    plane_cos, plane_sin, depth_cos, depth_sin, hermite = phase_tables(band_size, SHIFTS)
    plane_cos = plane_cos.astype(jnp.bfloat16)
    plane_sin = plane_sin.astype(jnp.bfloat16)
    depth_cos = depth_cos.astype(jnp.bfloat16)
    depth_sin = depth_sin.astype(jnp.bfloat16)
    signal = jnp.transpose(
        records.astype(jnp.float32).reshape(pair_count, 2, band_size, band_size, half_band),
        (1, 2, 3, 4, 0),
    )
    template = jnp.transpose(
        references.astype(jnp.float32).reshape(pair_count, 2, band_size, band_size, half_band),
        (1, 2, 3, 4, 0),
    )
    coverage = jnp.transpose(wedges, (1, 2, 0))[:, None, :, :]
    prod_real = (coverage * (signal[0] * template[0] + signal[1] * template[1])).astype(
        jnp.bfloat16
    )
    prod_imag = (coverage * (signal[0] * template[1] - signal[1] * template[0])).astype(
        jnp.bfloat16
    )
    weighting = hermite[None, None, :, None] * coverage
    signal_norm = jnp.sum(
        weighting * (signal[0] * signal[0] + signal[1] * signal[1]), axis=(0, 1, 2)
    )
    template_norm = jnp.sum(
        weighting * (template[0] * template[0] + template[1] * template[1]), axis=(0, 1, 2)
    )
    first_real, first_imag = section("abcn,as->sbcn", prod_real, prod_imag, plane_cos, plane_sin)
    second_real, second_imag = section(
        "sbcn,bt->stcn",
        first_real.astype(jnp.bfloat16),
        first_imag.astype(jnp.bfloat16),
        plane_cos,
        plane_sin,
    )
    correlation = multiply("stcn,cu->stun", second_real.astype(jnp.bfloat16), depth_cos) - multiply(
        "stcn,cu->stun", second_imag.astype(jnp.bfloat16), depth_sin
    )
    summit = jnp.max(correlation.reshape(-1, pair_count), axis=0)
    return score_gain * summit * lax.rsqrt(signal_norm * template_norm + 1e-06)


def score_pairs(records, panel_table, wedges, indices, block_limit):
    row_count = indices.shape[0]
    tried_count = indices.shape[1]
    pair_count = row_count * tried_count
    block_size = math.gcd(pair_count, block_limit)
    flat_index = indices.reshape(pair_count)

    def one_block(block_index):
        start_pair = block_index * block_size
        source_rows = (start_pair + jnp.arange(block_size, dtype=jnp.int32)) // tried_count
        return correlate(
            jnp.take(records, source_rows, axis=0),
            jnp.take(panel_table, flat_index, axis=0),
            jnp.take(wedges, source_rows, axis=0),
        )

    blocks = jnp.arange(pair_count // block_size, dtype=jnp.int32)
    return lax.map(one_block, blocks).reshape(row_count, tried_count)


def renew(tables, numerator, denominator):
    entries = tables.shape[0]
    band_size = tables.shape[1] // 2
    half_band = band_size // 2
    summed = (tables.astype(jnp.float32) + numerator).reshape(
        entries, 2, band_size, band_size, half_band
    )
    divisor = 1.0 + denominator.reshape(entries, 1, band_size, 1, half_band)
    return (summed / divisor).reshape(tables.shape).astype(jnp.bfloat16)


def route_matrix(class_now, owners, capacity):
    row_total = class_now.shape[0]
    position = jnp.arange(row_total, dtype=jnp.int32)
    earlier = (class_now[:, None] == class_now[None, :]) & (position[None, :] < position[:, None])
    ranking = jnp.sum(earlier.astype(jnp.int32), axis=1)
    target = class_now * capacity + ranking
    slot_ids = jnp.arange(owners * capacity, dtype=jnp.int32)
    return jnp.where(slot_ids[:, None] == target[None, :], 1.0, 0.0).astype(jnp.bfloat16)


def pack_rows(routing, particles, orient_now, tilt_low, tilt_high, weight_now, owners, capacity):
    records = jnp.einsum(
        "sp,pab->sab", routing, particles, preferred_element_type=jnp.float32
    ).astype(jnp.bfloat16)
    integers = jnp.concatenate([orient_now, tilt_low[:, None], tilt_high[:, None]], axis=1).astype(
        jnp.bfloat16
    )
    labels = jnp.dot(routing, integers, preferred_element_type=jnp.float32).astype(jnp.int32)
    shares = jnp.dot(
        routing, weight_now.astype(jnp.bfloat16), preferred_element_type=jnp.float32
    ).astype(jnp.bfloat16)
    return (
        records.reshape((owners, capacity) + records.shape[1:]),
        labels.reshape(owners, capacity, labels.shape[1]),
        shares.reshape(owners, capacity, shares.shape[1]),
    )


def shards(particles, panels, classes, candidates, weights, tilt_low, tilt_high):
    owners = lax.axis_size("cls")
    capacity = 2 * particles.shape[0] // owners
    band_size = particles.shape[1] // 2
    half_band = band_size // 2
    own_panels = panels[0]
    slot_total = owners * capacity
    routes = [
        route_matrix(classes[iteration, :, 0], owners, capacity) for iteration in range(ITERS)
    ]

    def pack_step(iteration):
        return pack_rows(
            routes[iteration],
            particles,
            candidates[iteration],
            tilt_low,
            tilt_high,
            weights[iteration],
            owners,
            capacity,
        )

    packed = [pack_step(iteration) for iteration in range(ITERS)]
    record_all, label_all, share_all = (
        lax.all_to_all(
            jnp.stack([bundle[0] for bundle in packed], 1),
            "cls",
            split_axis=0,
            concat_axis=0,
            tiled=True,
        ),
        lax.all_to_all(
            jnp.stack([bundle[1] for bundle in packed], 1),
            "cls",
            split_axis=0,
            concat_axis=0,
            tiled=True,
        ),
        lax.all_to_all(
            jnp.stack([bundle[2] for bundle in packed], 1),
            "cls",
            split_axis=0,
            concat_axis=0,
            tiled=True,
        ),
    )
    gathered = None
    results = []
    for iteration in range(ITERS):
        arrived = (record_all[:, iteration], label_all[:, iteration], share_all[:, iteration])
        records = arrived[0].reshape((slot_total,) + arrived[0].shape[2:])
        labels = arrived[1].reshape(slot_total, NCAND + 2)
        shares = arrived[2].reshape(slot_total, NCAND)
        orient_slots = labels[:, :NCAND]
        wedges = wedge_mask(labels[:, NCAND], labels[:, NCAND + 1], band_size)
        gathered = lax.all_gather(own_panels, "rot", axis=0, tiled=True)
        slot_scores = score_pairs(records, gathered, wedges, orient_slots, 256)
        returned = lax.all_to_all(
            slot_scores.reshape(owners, capacity, NCAND),
            "cls",
            split_axis=0,
            concat_axis=0,
            tiled=True,
        )
        results.append(
            jnp.einsum(
                "sp,sj->pj",
                routes[iteration].astype(jnp.float32),
                returned.reshape(slot_total, NCAND),
                precision=highest,
            )
        )
        spread = (
            jnp.broadcast_to(wedges[:, :, None, :], (slot_total, band_size, band_size, half_band))
            .reshape(slot_total, band_size, band_size * half_band)
            .astype(jnp.bfloat16)
        )
        masked = records * jnp.concatenate([spread, spread], axis=1)
        orient_range = jnp.arange(ORIENT, dtype=jnp.int32)
        selector = jnp.sum(
            jnp.where(
                orient_slots[:, :, None] == orient_range[None, None, :],
                shares.astype(jnp.float32)[:, :, None],
                0.0,
            ),
            axis=1,
        ).astype(jnp.bfloat16)
        numer_term = jnp.einsum("so,sab->oab", selector, masked, preferred_element_type=jnp.float32)
        cover_flat = wedges.reshape(slot_total, band_size * half_band).astype(jnp.bfloat16)
        denom_term = jnp.einsum(
            "so,sc->oc", selector, cover_flat, preferred_element_type=jnp.float32
        )
        numer_own, denom_own = (
            lax.psum_scatter(
                numer_term.astype(jnp.bfloat16), "rot", scatter_dimension=0, tiled=True
            ).astype(jnp.float32),
            lax.psum_scatter(
                denom_term.astype(jnp.bfloat16), "rot", scatter_dimension=0, tiled=True
            ).astype(jnp.float32),
        )
        own_panels = renew(own_panels, numer_own, denom_own)
        gathered = None
    return (jnp.stack(results), own_panels[None])


def rounded_tables(band_size, shift_count):
    plane_cos, plane_sin, depth_cos, depth_sin, hermite = phase_tables(band_size, shift_count)
    return tuple(
        table.astype(jnp.bfloat16) for table in (plane_cos, plane_sin, depth_cos, depth_sin)
    )


def stage_matrices(band_size, shift_count, block):
    plane_cos, plane_sin, depth_cos, depth_sin = rounded_tables(band_size, shift_count)
    half_band = band_size // 2
    turn = jnp.stack(
        [jnp.stack([plane_cos, plane_sin], 0), jnp.stack([-plane_sin, plane_cos], 0)], 0
    )
    each = jnp.eye(block, dtype=jnp.bfloat16)
    over_kx = jnp.einsum("icas,pq->cpsqia", turn, each).reshape(
        2 * block * shift_count, block * 2 * band_size
    )
    depth_eye = jnp.eye(half_band, dtype=jnp.bfloat16)
    over_ky = jnp.einsum("icbt,kl->ibkctl", turn, depth_eye).reshape(
        2 * band_size * half_band, 2 * shift_count * half_band
    )
    depth = jnp.stack([depth_cos, -depth_sin], 0)
    shift_eye = jnp.eye(shift_count, dtype=jnp.bfloat16)
    over_kz = jnp.einsum("iku,tv->itkvu", depth, shift_eye).reshape(
        2 * shift_count * half_band, shift_count * shift_count
    )
    return over_kx, over_ky, over_kz


def wedge_grid(band_size, lanes):
    half_band = band_size // 2
    across = lax.broadcasted_iota(jnp.int32, (band_size, lanes), 0) - band_size // 2
    depth = lax.broadcasted_iota(jnp.int32, (band_size, lanes), 1) % half_band
    flipped = across < 0
    across_abs = jnp.where(flipped, -across, across).astype(jnp.float32)
    along = (8 * jnp.where(flipped, -depth, depth)).astype(jnp.float32)
    hermite = jnp.where(depth == 0, 1.0, 2.0).astype(jnp.float32)
    return across_abs, along, hermite


def slot_mask(info_ref, slot, across, along):
    low_ok = info_ref[NCAND, slot] * across <= along
    high_ok = along <= info_ref[NCAND + 1, slot] * across
    return jnp.where(low_ok & high_ok, 1.0, 0.0).astype(jnp.float32)


def score_kernel(
    index_ref,
    info_ref,
    record_ref,
    panel_ref,
    kx_ref,
    ky_ref,
    kz_ref,
    score_ref,
    product_ref,
    own_ref,
    other_ref,
    summit_ref,
    *,
    block,
):
    slots, rows, lanes = record_ref.shape
    band_size = rows // 2
    across, along, hermite = wedge_grid(band_size, lanes)

    def one_slot(slot, carry):
        mask = slot_mask(info_ref, slot, across, along)
        record = record_ref[slot].astype(jnp.float32)
        real, imag = mask * record[:band_size], mask * record[band_size:]
        own_ref[pl.ds(slot, 1), :] = jnp.sum(
            hermite * (real * real + imag * imag), axis=0, keepdims=True
        )
        weighting = hermite * mask
        for tried in range(NCAND):
            panel = panel_ref[index_ref[tried, slot]].astype(jnp.float32)
            panel_real, panel_imag = panel[:band_size], panel[band_size:]
            product_ref[pl.ds(slot * rows, band_size), tried * lanes : (tried + 1) * lanes] = (
                real * panel_real + imag * panel_imag
            ).astype(jnp.bfloat16)
            product_ref[
                pl.ds(slot * rows + band_size, band_size), tried * lanes : (tried + 1) * lanes
            ] = (real * panel_imag - imag * panel_real).astype(jnp.bfloat16)
            other_ref[tried, pl.ds(slot, 1), :] = jnp.sum(
                weighting * (panel_real * panel_real + panel_imag * panel_imag),
                axis=0,
                keepdims=True,
            )
        return carry

    lax.fori_loop(0, slots, one_slot, 0, unroll=math.gcd(slots, 8))

    span = block * rows

    def one_block(number, carry):
        product = product_ref[pl.ds(pl.multiple_of(number * span, span), span), :]
        first = jnp.dot(kx_ref[...], product, preferred_element_type=jnp.float32).astype(
            jnp.bfloat16
        )
        half = first.shape[0] // 2
        lefts = [
            jnp.concatenate(
                [
                    first[:half, tried * lanes : (tried + 1) * lanes],
                    first[half:, tried * lanes : (tried + 1) * lanes],
                ],
                axis=1,
            )
            for tried in range(NCAND)
        ]
        left = jnp.concatenate(lefts, axis=0)
        second = jnp.dot(left, ky_ref[...], preferred_element_type=jnp.float32).astype(jnp.bfloat16)
        corr = jnp.dot(second, kz_ref[...], preferred_element_type=jnp.float32)
        for tried in range(NCAND):
            part = corr[tried * half : (tried + 1) * half]
            best = part[:, :lanes]
            for start in range(lanes, part.shape[1], lanes):
                best = jnp.maximum(best, part[:, start : start + lanes])
            best = jnp.max(best.reshape(block, half // block, lanes), axis=1)
            summit_ref[tried, pl.ds(pl.multiple_of(number * block, block), block), :] = best
        return carry

    blocks = slots // block
    lax.fori_loop(0, blocks, one_block, 0, unroll=math.gcd(blocks, 4))
    own = jnp.sum(own_ref[...], axis=1, keepdims=True)
    lane = lax.broadcasted_iota(jnp.int32, (slots, lanes), 1)
    result = jnp.zeros((slots, lanes), jnp.float32)
    for tried in range(NCAND):
        other = jnp.sum(other_ref[tried], axis=1, keepdims=True)
        summit = jnp.max(summit_ref[tried], axis=1, keepdims=True)
        result = jnp.where(
            lane == tried, score_gain * summit * lax.rsqrt(own * other + 1e-06), result
        )
    score_ref[...] = result


def update_kernel(index_ref, info_ref, record_ref, panel_ref, out_ref, numer_ref, denom_ref):
    slots, rows, lanes = record_ref.shape
    band_size = rows // 2
    across, along, hermite = wedge_grid(band_size, lanes)
    numer_ref[...] = jnp.zeros_like(numer_ref)
    denom_ref[...] = jnp.zeros_like(denom_ref)

    def one_slot(slot, carry):
        mask = slot_mask(info_ref, slot, across, along)
        record = record_ref[slot].astype(jnp.float32)
        masked = jnp.concatenate([mask, mask], axis=0) * record
        for tried in range(NCAND):
            where = index_ref[tried, slot]
            share = info_ref[NCAND + 2 + tried, slot]
            numer_ref[where] = numer_ref[where] + share * masked
            denom_ref[where] = denom_ref[where] + share * mask
        return carry

    lax.fori_loop(0, slots, one_slot, 0, unroll=math.gcd(slots, 4))

    def one_panel(entry, carry):
        numer = numer_ref[entry].astype(jnp.bfloat16).astype(jnp.float32)
        denom = 1.0 + denom_ref[entry].astype(jnp.bfloat16).astype(jnp.float32)
        summed = panel_ref[entry].astype(jnp.float32) + numer
        out_ref[entry] = (summed / jnp.concatenate([denom, denom], axis=0)).astype(jnp.bfloat16)
        return carry

    entries = panel_ref.shape[0]
    lax.fori_loop(0, entries, one_panel, 0, unroll=math.gcd(entries, 4))


smem_spec = pl.BlockSpec(memory_space=pltpu.SMEM)
vmem_spec = pl.BlockSpec(memory_space=pltpu.VMEM)
kernel_grant = 24 << 20


def score_slots(index, info, records, panels, matrices, block):
    slots, rows, lanes = records.shape
    flops = 3 * 2 * slots * NCAND * 16 * 256 * 256
    return pl.pallas_call(
        functools.partial(score_kernel, block=block),
        out_shape=jax.ShapeDtypeStruct((slots, lanes), jnp.float32),
        in_specs=[smem_spec, smem_spec] + [vmem_spec] * 5,
        out_specs=vmem_spec,
        scratch_shapes=[
            pltpu.VMEM((slots * rows, NCAND * lanes), jnp.bfloat16),
            pltpu.VMEM((slots, lanes), jnp.float32),
            pltpu.VMEM((NCAND, slots, lanes), jnp.float32),
            pltpu.VMEM((NCAND, slots, lanes), jnp.float32),
        ],
        compiler_params=pltpu.CompilerParams(vmem_limit_bytes=kernel_grant),
        cost_estimate=pl.CostEstimate(
            flops=flops, bytes_accessed=16 << 20, transcendentals=0
        ),
        name="score",
    )(index, info, records, panels, *matrices)


def update_panels(index, info, records, panels):
    slots, rows, lanes = records.shape
    entries = panels.shape[0]
    return pl.pallas_call(
        update_kernel,
        out_shape=jax.ShapeDtypeStruct(panels.shape, panels.dtype),
        in_specs=[smem_spec, smem_spec] + [vmem_spec] * 2,
        out_specs=vmem_spec,
        scratch_shapes=[
            pltpu.VMEM((entries, rows, lanes), jnp.float32),
            pltpu.VMEM((entries, rows // 2, lanes), jnp.float32),
        ],
        compiler_params=pltpu.CompilerParams(vmem_limit_bytes=kernel_grant),
        cost_estimate=pl.CostEstimate(
            flops=1 << 20, bytes_accessed=16 << 20, transcendentals=0
        ),
        name="update",
    )(index, info, records, panels)


def exchange(values):
    return lax.all_to_all(values, "cls", split_axis=0, concat_axis=0, tiled=True)


def owner_shards(particles, panels, classes, candidates, weights, tilt_low, tilt_high):
    owners = lax.axis_size("cls")
    capacity = 2 * particles.shape[0] // owners
    rows, lanes = particles.shape[1:]
    band_size = rows // 2
    block = 8
    slot_total = owners * capacity
    own_panels = panels[0]
    routes = [
        route_matrix(classes[iteration, :, 0], owners, capacity) for iteration in range(ITERS)
    ]
    arrived = []
    info_count = 2 * NCAND + 2
    for iteration in range(ITERS):
        info = jnp.concatenate(
            [
                candidates[iteration].astype(jnp.bfloat16),
                tilt_low[:, None].astype(jnp.bfloat16),
                tilt_high[:, None].astype(jnp.bfloat16),
                weights[iteration].astype(jnp.bfloat16),
            ],
            axis=1,
        )
        carried = particles.at[:, band_size // 2, 1 : 1 + info_count].set(info)
        packed = jnp.einsum(
            "sp,pab->sab", routes[iteration], carried, preferred_element_type=jnp.float32
        ).astype(jnp.bfloat16)
        arrived.append(
            exchange(packed.reshape(owners, capacity, rows, lanes)).reshape(slot_total, rows, lanes)
        )
    matrices = stage_matrices(band_size, SHIFTS, block)
    scored = []
    for iteration in range(ITERS):
        records = arrived[iteration]
        info = records[:, band_size // 2, 1 : 1 + info_count].astype(jnp.float32).T
        index = info[:NCAND].astype(jnp.int32)
        scored.append(score_slots(index, info, records, own_panels, matrices, block)[:, :NCAND])
        own_panels = update_panels(index, info, records, own_panels)
    returned = exchange(jnp.stack(scored, 1).reshape(owners, capacity, ITERS, NCAND)).reshape(
        slot_total, ITERS, NCAND
    )
    results = [
        jnp.einsum(
            "sp,sj->pj",
            routes[iteration].astype(jnp.float32),
            returned[:, iteration],
            precision=highest,
        )
        for iteration in range(ITERS)
    ]
    return (jnp.stack(results), own_panels[None])


def solution(mesh):
    placed = (
        P(("cls", "rot"), None, None),
        P("cls", "rot", None, None),
        P(None, ("cls", "rot"), None),
        P(None, ("cls", "rot"), None),
        P(None, ("cls", "rot"), None),
        P(("cls", "rot")),
        P(("cls", "rot")),
    )
    return jax.shard_map(
        owner_shards if mesh.shape["rot"] == 1 else shards,
        mesh=mesh,
        in_specs=placed,
        out_specs=(P(None, ("cls", "rot"), None), P("cls", "rot", None, None)),
        check_vma=False,
    )
```
